32 devices in a mesh: crop: 8 (over z, x), shard: 4 (over y, core).
Axes of the slice: x: 2, y: 2, z: 4, core: 2. Of those that a mesh axis runs over, the one named last changes fastest.
Arguments:
- master: float32 [14320, 128], P('shard')
- first_moment: float32 [14320, 128], P('shard'), may hold values from -5.722046e-06 to 5.722046e-06
- second_moment: float32 [14320, 128], P('shard'), may hold values from 6.8195707e-15 to 1.0911313e-13
- step: int32 [1], replicated, may hold values from 2 to 20
- plm_table: bfloat16 [21, 1280], replicated, may hold values from -6 to 6
- plm_first: bfloat16 [1280, 5248], P('shard'), may hold values from -0.15625 to 0.15625
- plm_second: bfloat16 [2560, 1280], P('shard'), may hold values from -0.25 to 0.25
- tokens: int32 [512, 32], P(('crop', 'shard')), may hold values from 0 to 20
- lengths: int32 [512], P(('crop', 'shard')), may hold values from 12 to 32
- resolved: int32 [512, 32], P(('crop', 'shard')), may hold values 0 or 1
- coords: float32 [512, 3, 32], P(('crop', 'shard')), may hold values from -15 to 15
Outputs:
- new_master: float32 [14320, 128], P('shard')
- new_first: float32 [14320, 128], P('shard')
- new_second: float32 [14320, 128], P('shard')
- weights_low: bfloat16 [14320, 128], P('shard')
- loss: float32 [], replicated
- grad_norm: float32 [], replicated
The draws below stay inside these ranges and needn't reach their ends.
All inputs are finite; a program needn't handle non-finite values. No bound on the sum of `resolved` on one device may be relied on, other than what follows from the above.
Results may differ from the reference program's by a relative error of at most 0.012.
The reference program's roundings to bfloat16 on the way count: a program that leaves them out, or rounds other values in their place, can miss the bound.
Values may be sent and summed in bfloat16 or wider, within the bound.
No kernel may reach another device: no remote copies, remote signals or barrier semaphores. Data moves between devices by JAX's collectives and lax.ppermute only.
A program may use at most 320 MiB of HBM per device.

```python
import math
import jax
import jax.numpy as jnp
from jax import lax

NODE = 256
PAIR = 128
HEADS = 8
PAIR_HEADS = 4
PLM = 1280
PLM_FF = 2560
PLM_Z = 128
NODE_FF = 1024
PAIR_FF = 512
VOCAB = 21
BINS = 65
IPA_PTS = 4
RES = 32
MIN_LEN = 12
MICRO = 4
CROPS_MB = 4
CROPS = 512
RAWPARAM = 1832832
NPARAM = 1832960
PROWS = 14320
DEVICES = 32


def draw_master(key, part):
    segments = [((PLM, NODE), PLM ** (-0.5)), ((NODE, 3 * NODE), NODE ** (-0.5)), ((NODE, NODE), (NODE // 16) ** (-0.5)), ((NODE, 2 * PAIR), NODE ** (-0.5)), ((NODE, NODE_FF), NODE ** (-0.5)), ((NODE_FF, NODE), NODE_FF ** (-0.5)), ((PAIR, HEADS), PAIR ** (-0.5)), ((PAIR, PAIR), PAIR ** (-0.5)), ((PAIR, 5 * PAIR), PAIR ** (-0.5)), ((PAIR, PAIR), PAIR ** (-0.5)), ((PAIR, 4 * PAIR), PAIR ** (-0.5)), ((PAIR, PAIR), (PAIR // 16) ** (-0.5)), ((PAIR, PAIR_FF), PAIR ** (-0.5)), ((PAIR_FF, PAIR), PAIR_FF ** (-0.5)), ((BINS, PAIR), 1.0), ((NODE, 3), 3.0 * NODE ** (-0.5)), ((NODE, 3 * NODE), NODE ** (-0.5)), ((NODE, 6 * HEADS * IPA_PTS), NODE ** (-0.5)), ((PAIR, HEADS), PAIR ** (-0.5)), ((NODE, NODE), (NODE // 16) ** (-0.5)), ((NODE, 3), 3.0 * NODE ** (-0.5))]
    pieces = []
    for index, (extent, scale) in enumerate(segments):
        sub_key = jax.random.fold_in(key, index)
        pieces.append(jax.random.truncated_normal(sub_key, -4.0, 4.0, (extent[0] * extent[1],), jnp.float32) * scale)
    gain_key = jax.random.fold_in(key, 100)
    pieces.append(1.0 + jax.random.uniform(gain_key, (6 * NODE + 6 * PAIR,), jnp.float32, -0.3, 0.3))
    spare_key = jax.random.fold_in(key, 200)
    pieces.append(jax.random.truncated_normal(spare_key, -4.0, 4.0, (NPARAM - RAWPARAM,), jnp.float32) * 0.05)
    return jnp.concatenate(pieces).reshape(PROWS, 128)


def draw_lengths(key, part):
    crop_index = jnp.arange(CROPS, dtype=jnp.int32)
    device_index = crop_index // (MICRO * CROPS_MB)
    base = MIN_LEN + (RES - MIN_LEN) * device_index // max(DEVICES - 1, 1)
    jitter = jax.random.randint(jax.random.fold_in(key, 7), (CROPS,), -2, 3, dtype=jnp.int32)
    drawn = jnp.clip(base + jitter, MIN_LEN, RES)
    drawn = jnp.where(crop_index == 0, MIN_LEN, drawn)
    drawn = jnp.where(crop_index == CROPS - 1, RES, drawn)
    return drawn.astype(jnp.int32)


def plant(values, stream_key, least, top_value):
    index_at = [jax.random.randint(jax.random.fold_in(stream_key, axis), (), 0, length) for axis, length in enumerate(values.shape)]
    longest = values.shape.index(max(values.shape))
    next_to = index_at[:longest] + [(index_at[longest] + 1) % values.shape[longest]] + index_at[longest + 1:]
    return values.at[tuple(index_at)].set(least).at[tuple(next_to)].set(top_value)


def block_levels(key, dims, split, least, largest):
    loudness = 1.0
    for dim, blocks in split:
        heights = jax.random.uniform(jax.random.fold_in(jax.random.fold_in(key, 6), dim), (blocks,), jnp.float32, least / len(split), largest / len(split))
        loudness = loudness * jnp.repeat(jnp.exp(heights), dims[dim] // blocks).reshape((-1,) + (1,) * (len(dims) - 1 - dim))
    return loudness


def noise(stream_key, shape, deviation, most, shards=(), kind=jnp.bfloat16):
    loudness = block_levels(stream_key, shape, shards, -0.22, 0.18) if shards else 1.0
    result = jax.random.normal(stream_key, shape, jnp.float32) * deviation * loudness
    return jnp.minimum(jnp.maximum(result, -most), most).astype(kind)


def setup_inputs(seed: int = 0) -> dict:
    arg_keys = jax.random.split(jax.random.key(seed), 12)
    return {
        "master": draw_master(jax.random.fold_in(arg_keys[11], 71), 0),
        "first_moment": noise(arg_keys[1], (PROWS, 128), (0.11 * 0.005 / NPARAM ** 0.5), 5.7220458984375e-06, ((0, 4),), jnp.float32),
        "second_moment": jnp.clip(jnp.exp(math.log(1.0911313085698593e-13) - 2.7725887 * jax.random.uniform(arg_keys[2], (PROWS, 128), jnp.float32) ** block_levels(arg_keys[2], (PROWS, 128), ((0, 4),), -0.2, 0.2)), 6.8195706785616206e-15, 1.0911313085698593e-13),
        "step": jax.random.randint(arg_keys[3], (1,), 2, 21).astype(jnp.int32),
        "plm_table": noise(arg_keys[4], (VOCAB, PLM), 1.0, 6.0),
        "plm_first": noise(arg_keys[5], (PLM, 2 * PLM_FF + PLM_Z), PLM ** -0.5, 0.15625, ((0, 4),)),
        "plm_second": noise(arg_keys[6], (PLM_FF, PLM), (PLM_FF // 4) ** -0.5, 0.25, ((0, 4),)),
        "tokens": plant(jax.random.randint(arg_keys[7], (CROPS, RES), 0, VOCAB), jax.random.fold_in(arg_keys[7], 1), 0, VOCAB - 1).astype(jnp.int32),
        "lengths": draw_lengths(jax.random.fold_in(arg_keys[11], 71), 0),
        "resolved": plant((jax.random.randint(arg_keys[9], (CROPS, RES), 0, 10) < 9).astype(jnp.int32), jax.random.fold_in(arg_keys[9], 1), 0, 1),
        "coords": noise(arg_keys[10], (CROPS, 3, RES), 3.0, 15.0, ((0, 32),), jnp.float32),
    }


@jax.custom_vjp
def low(v):
    return lax.optimization_barrier(v.astype(jnp.bfloat16)).astype(jnp.float32)

@jax.custom_vjp
def low_back(v):
    return v

def low_keep(v):
    return (low(v), None)

def low_pass(kept, grad):
    return (grad,)

def back_keep(v):
    return (v, None)

def back_low(kept, grad):
    return (low(grad),)
low.defvjp(low_keep, low_pass)
low_back.defvjp(back_keep, back_low)
beta_one = 0.9
beta_two = 0.999
learn_rate = 0.02
adam_eps = 1e-10
decay_rate = 0.01
clip_norm = 0.005
point_weight = 0.01

def layout():
    return [('w_in', (PLM, NODE)), ('w_qkv', (NODE, 3 * NODE)), ('w_out', (NODE, NODE)), ('w_lr', (NODE, 2 * PAIR)), ('w_n1', (NODE, NODE_FF)), ('w_n2', (NODE_FF, NODE)), ('w_bias', (PAIR, HEADS)), ('w_op', (PAIR, PAIR)), ('w_tri', (PAIR, 5 * PAIR)), ('w_tri_out', (PAIR, PAIR)), ('w_pa', (PAIR, 4 * PAIR)), ('w_pa_out', (PAIR, PAIR)), ('w_p1', (PAIR, PAIR_FF)), ('w_p2', (PAIR_FF, PAIR)), ('w_rel', (BINS, PAIR)), ('w_s', (NODE, 3)), ('w_ipa', (NODE, 3 * NODE)), ('w_pts', (NODE, 6 * HEADS * IPA_PTS)), ('w_ipa_bias', (PAIR, HEADS)), ('w_ipa_out', (NODE, NODE)), ('w_bb', (NODE, 3)), ('g_node', (6, NODE)), ('g_pair', (6, PAIR))]

def unpack(flat):
    params = {}
    offset = 0
    for weight_name, extent in layout():
        entries = extent[0] * extent[1]
        params[weight_name] = flat[offset:offset + entries].reshape(extent)
        offset += entries
    return params

def product(form, left, right):
    return jnp.einsum(form, left, right, precision=lax.Precision.HIGHEST)

def rounded(values):
    return low_back(low(values))

def layer_norm(values, gain):
    centred = values - lax.optimization_barrier(jnp.mean(values, axis=-1, keepdims=True))
    spread = lax.optimization_barrier(jnp.mean(centred * centred, axis=-1, keepdims=True))
    return centred * lax.rsqrt(spread + 1e-05) * gain

def softmax_last(scores):
    expo = jnp.exp(scores - lax.optimization_barrier(jnp.max(scores, axis=-1, keepdims=True)))
    return expo / lax.optimization_barrier(jnp.sum(expo, axis=-1, keepdims=True))

def residue_weight(lengths, resolved):
    positions = jnp.arange(resolved.shape[1])
    valid = (positions[None, :] < lengths[:, None]).astype(jnp.float32)
    first = (positions == 0).astype(jnp.float32)[None, :]
    return (jnp.maximum(resolved.astype(jnp.float32), first) * valid, valid)

def crop_loss(params, table, plm_first, plm_second, tokens, lengths, resolved, coords, inv_count, multiply, round_fn):
    crops, residues = tokens.shape
    positions = jnp.arange(residues)
    weight_res, valid = residue_weight(lengths, resolved)
    key_mask = valid[:, None, :] > 0
    pmask = (valid[:, :, None] * valid[:, None, :])[..., None]
    one_hot = (tokens[:, :, None] == jnp.arange(VOCAB)[None, None, :]).astype(jnp.float32)
    features = multiply('crv,vp->crp', one_hot, table)
    uvz = jax.nn.silu(multiply('crp,pe->cre', round_fn(layer_norm(features, 1.0)), plm_first))
    base = round_fn(uvz[..., 2 * PLM_FF:])
    plm_scores = jnp.where(key_mask, multiply('ciz,cjz->cij', base, base) * PLM_Z ** (-0.5), -1000000000.0)
    mixed = multiply('cij,cje->cie', round_fn(softmax_last(plm_scores)), round_fn(uvz[..., PLM_FF:2 * PLM_FF]))
    plm_out = features + multiply('cie,ep->cip', round_fn(uvz[..., :PLM_FF] * mixed), plm_second)
    node = multiply('crp,pn->crn', round_fn(layer_norm(plm_out, 1.0)), params['w_in'])
    offsets = jnp.clip(positions[None, :] - positions[:, None] + (BINS - 1) // 2, 0, BINS - 1)
    rel_hot = (offsets[:, :, None] == jnp.arange(BINS)[None, None, :]).astype(jnp.float32)
    pair = jnp.broadcast_to(multiply('ijb,bp->ijp', rel_hot, params['w_rel'])[None], (crops, residues, residues, PAIR))
    gain_node, gain_pair = (params['g_node'], params['g_pair'])
    sides = multiply('crn,nq->crq', round_fn(layer_norm(node, gain_node[0])), params['w_lr'])
    outer = sides[:, :, None, :PAIR] * sides[:, None, :, PAIR:]
    pair = pair + multiply('cijp,pq->cijq', round_fn(outer), params['w_op'])
    tri_proj = multiply('cijp,pq->cijq', round_fn(layer_norm(pair, gain_pair[0])), params['w_tri'])
    tri_left = jax.nn.sigmoid(tri_proj[..., :PAIR]) * tri_proj[..., PAIR:2 * PAIR] * pmask
    tri_right = jax.nn.sigmoid(tri_proj[..., 2 * PAIR:3 * PAIR]) * tri_proj[..., 3 * PAIR:4 * PAIR] * pmask
    tri = multiply('cikp,cjkp->cijp', round_fn(tri_left), round_fn(tri_right))
    tri_update = multiply('cijp,pq->cijq', round_fn(layer_norm(tri, gain_pair[1])), params['w_tri_out'])
    pair = pair + jax.nn.sigmoid(tri_proj[..., 4 * PAIR:]) * tri_update
    pair_dim = PAIR // PAIR_HEADS
    pa_proj = multiply('cijp,pq->cijq', round_fn(layer_norm(pair, gain_pair[2])), params['w_pa'])
    pa_qkv = round_fn(pa_proj[..., :3 * PAIR])
    pa_query = pa_qkv[..., :PAIR].reshape(crops, residues, residues, PAIR_HEADS, pair_dim)
    pa_keys = pa_qkv[..., PAIR:2 * PAIR].reshape(crops, residues, residues, PAIR_HEADS, pair_dim)
    pa_values = pa_qkv[..., 2 * PAIR:].reshape(crops, residues, residues, PAIR_HEADS, pair_dim)
    pa_scores = multiply('cijhd,cikhd->cihjk', pa_query, pa_keys) * pair_dim ** (-0.5)
    pa_scores = jnp.where(valid[:, None, None, None, :] > 0, pa_scores, -1000000000.0)
    pa_out = multiply('cihjk,cikhd->cijhd', round_fn(softmax_last(pa_scores)), pa_values).reshape(crops, residues, residues, PAIR)
    pair = pair + multiply('cijp,pq->cijq', round_fn(jax.nn.sigmoid(pa_proj[..., 3 * PAIR:]) * pa_out), params['w_pa_out'])
    hidden = jax.nn.gelu(multiply('cijp,pf->cijf', round_fn(layer_norm(pair, gain_pair[3])), params['w_p1']), approximate=True)
    pair = pair + multiply('cijf,fp->cijp', round_fn(hidden), params['w_p2'])
    bias = multiply('cijp,ph->chij', round_fn(layer_norm(pair, gain_pair[4])), params['w_bias'])
    head_dim = NODE // HEADS
    qkv = round_fn(multiply('crn,nq->crq', round_fn(layer_norm(node, gain_node[1])), params['w_qkv']))
    query = qkv[..., :NODE].reshape(crops, residues, HEADS, head_dim)
    keys = qkv[..., NODE:2 * NODE].reshape(crops, residues, HEADS, head_dim)
    values = qkv[..., 2 * NODE:].reshape(crops, residues, HEADS, head_dim)
    scores = multiply('cihd,cjhd->chij', query, keys) * head_dim ** (-0.5) + bias
    scores = jnp.where(valid[:, None, None, :] > 0, scores, -1000000000.0)
    attended = multiply('chij,cjhd->cihd', round_fn(softmax_last(scores)), values).reshape(crops, residues, NODE)
    node = node + multiply('crn,nm->crm', round_fn(attended), params['w_out'])
    hidden_node = jax.nn.gelu(multiply('crn,nf->crf', round_fn(layer_norm(node, gain_node[2])), params['w_n1']), approximate=True)
    node = node + multiply('crf,fn->crn', round_fn(hidden_node), params['w_n2'])
    start_pos = multiply('crn,nk->crk', round_fn(layer_norm(node, gain_node[3])), params['w_s'])
    single = round_fn(layer_norm(node, gain_node[4]))
    sqkv = round_fn(multiply('crn,nq->crq', single, params['w_ipa']))
    s_query = sqkv[..., :NODE].reshape(crops, residues, HEADS, head_dim)
    s_keys = sqkv[..., NODE:2 * NODE].reshape(crops, residues, HEADS, head_dim)
    s_values = sqkv[..., 2 * NODE:].reshape(crops, residues, HEADS, head_dim)
    points = round_fn(multiply('crn,nq->crq', single, params['w_pts'])).reshape(crops, residues, 2, HEADS, IPA_PTS, 3)
    points = points + start_pos[:, :, None, None, None, :]
    point_diff = points[:, :, None, 0] - points[:, None, :, 1]
    dist = jnp.transpose(lax.optimization_barrier(jnp.sum(point_diff * point_diff, axis=(-1, -2))), (0, 3, 1, 2))
    ipa_bias = multiply('cijp,ph->chij', round_fn(layer_norm(pair, gain_pair[5])), params['w_ipa_bias'])
    ipa_scores = multiply('cihd,cjhd->chij', s_query, s_keys) * head_dim ** (-0.5) + ipa_bias - point_weight * dist
    ipa_scores = jnp.where(valid[:, None, None, :] > 0, ipa_scores, -1000000000.0)
    ipa_att = multiply('chij,cjhd->cihd', round_fn(softmax_last(ipa_scores)), s_values).reshape(crops, residues, NODE)
    node = node + multiply('crn,nm->crm', round_fn(ipa_att), params['w_ipa_out'])
    predicted = start_pos + multiply('crn,nk->crk', round_fn(layer_norm(node, gain_node[5])), params['w_bb'])
    truth = jnp.transpose(coords, (0, 2, 1))
    pred_diff = predicted[:, :, None, :] - predicted[:, None, :, :]
    true_diff = truth[:, :, None, :] - truth[:, None, :, :]
    dist_pred = jnp.sqrt(lax.optimization_barrier(jnp.sum(pred_diff * pred_diff, axis=-1)) + 1.0)
    dist_true = jnp.sqrt(lax.optimization_barrier(jnp.sum(true_diff * true_diff, axis=-1)) + 1.0)
    error = jnp.sqrt((dist_pred - dist_true) ** 2 + 1.0) - 1.0
    pair_weight = weight_res[:, :, None] * weight_res[:, None, :]
    return jnp.sum(pair_weight * error) * inv_count

def adam_update(master, first_moment, second_moment, step, grad, norm):
    clipped = grad * jnp.minimum(1.0, clip_norm / norm)
    first = beta_one * first_moment + (1.0 - beta_one) * clipped
    second = beta_two * second_moment + (1.0 - beta_two) * clipped * clipped
    step_count = step[0].astype(jnp.float32)
    first_hat = first / (1.0 - beta_one ** step_count)
    second_hat = second / (1.0 - beta_two ** step_count)
    updated = master - learn_rate * (first_hat / (jnp.sqrt(second_hat) + adam_eps) + decay_rate * master)
    return (updated, first, second, updated.astype(jnp.bfloat16))

def reference(master, first_moment, second_moment, step, plm_table, plm_first, plm_second, tokens, lengths, resolved, coords):
    table = plm_table.astype(jnp.float32)
    frozen_first = plm_first.astype(jnp.float32)
    frozen_second = plm_second.astype(jnp.float32)
    weight_res, valid = residue_weight(lengths, resolved)
    count = jnp.sum(lax.optimization_barrier(jnp.sum(weight_res, axis=1)) ** 2)
    inv_count = 1.0 / count
    per_group = MICRO * CROPS_MB
    batches = (tokens.reshape(DEVICES, per_group, RES), lengths.reshape(DEVICES, per_group), resolved.reshape(DEVICES, per_group, RES), coords.reshape(DEVICES, per_group, 3, RES))

    def group_step(carry, batch):
        group_tokens, group_lengths, group_resolved, group_coords = batch

        def loss_of(flat):
            params = unpack(low(flat).reshape(-1))
            return crop_loss(params, table, frozen_first, frozen_second, group_tokens, group_lengths, group_resolved, group_coords, inv_count, product, rounded)
        value, pullback = jax.vjp(loss_of, master)
        grad, = pullback(jnp.float32(1.0))
        return ((carry[0] + grad, carry[1] + value), None)
    start = (jnp.zeros(master.shape, jnp.float32), jnp.float32(0.0))
    (grad, loss), unused = lax.scan(group_step, start, batches)
    norm = jnp.sqrt(jnp.sum(grad * grad))
    updated, first, second, copy_low = adam_update(master, first_moment, second_moment, step, grad, norm)
    return (updated, first, second, copy_low, loss, norm)
```

```python
import jax
import jax.numpy as jnp
from jax import lax
from jax.experimental import pallas as pl
from jax.experimental.pallas import tpu as pltpu
from jax.sharding import PartitionSpec as P

NODE = 256
PAIR = 128
HEADS = 8
PAIR_HEADS = 4
PLM = 1280
PLM_FF = 2560
PLM_Z = 128
NODE_FF = 1024
PAIR_FF = 512
VOCAB = 21
BINS = 65
IPA_PTS = 4
RES = 32
MICRO = 4


beta_one = 0.9
beta_two = 0.999
learn_rate = 0.02
adam_eps = 1e-10
decay_rate = 0.01
clip_norm = 0.005
point_weight = 0.01


BF = jnp.bfloat16
F32 = jnp.float32


def layout():
    return [
        ("w_in", (PLM, NODE)),
        ("w_qkv", (NODE, 3 * NODE)),
        ("w_out", (NODE, NODE)),
        ("w_lr", (NODE, 2 * PAIR)),
        ("w_n1", (NODE, NODE_FF)),
        ("w_n2", (NODE_FF, NODE)),
        ("w_bias", (PAIR, HEADS)),
        ("w_op", (PAIR, PAIR)),
        ("w_tri", (PAIR, 5 * PAIR)),
        ("w_tri_out", (PAIR, PAIR)),
        ("w_pa", (PAIR, 4 * PAIR)),
        ("w_pa_out", (PAIR, PAIR)),
        ("w_p1", (PAIR, PAIR_FF)),
        ("w_p2", (PAIR_FF, PAIR)),
        ("w_rel", (BINS, PAIR)),
        ("w_s", (NODE, 3)),
        ("w_ipa", (NODE, 3 * NODE)),
        ("w_pts", (NODE, 6 * HEADS * IPA_PTS)),
        ("w_ipa_bias", (PAIR, HEADS)),
        ("w_ipa_out", (NODE, NODE)),
        ("w_bb", (NODE, 3)),
        ("g_node", (6, NODE)),
        ("g_pair", (6, PAIR)),
    ]


def unpack(flat):
    params = {}
    offset = 0
    for weight_name, extent in layout():
        entries = extent[0] * extent[1]
        params[weight_name] = flat[offset : offset + entries].reshape(extent)
        offset += entries
    return params


def pack(params, total):
    flat = jnp.concatenate([params[weight_name].reshape(-1) for weight_name, extent in layout()])
    return jnp.pad(flat, (0, total - flat.shape[0])).reshape(-1, 128)


def product(form, left, right):
    return jnp.einsum(
        form,
        left.astype(jnp.bfloat16),
        right.astype(jnp.bfloat16),
        preferred_element_type=jnp.float32,
    )


def layer_norm(values, gain):
    centred = values - jnp.mean(values, axis=-1, keepdims=True)
    spread = jnp.mean(centred * centred, axis=-1, keepdims=True)
    return centred * lax.rsqrt(spread + 1e-05) * gain


def softmax_last(scores):
    expo = jnp.exp(scores - jnp.max(scores, axis=-1, keepdims=True))
    return expo / jnp.sum(expo, axis=-1, keepdims=True)


def residue_weight(lengths, resolved):
    positions = jnp.arange(resolved.shape[1])
    valid = (positions[None, :] < lengths[:, None]).astype(jnp.float32)
    first = (positions == 0).astype(jnp.float32)[None, :]
    return (jnp.maximum(resolved.astype(jnp.float32), first) * valid, valid)


PH = 4
RB = 8
M = RB * RES
EPS = 1e-05
NEG = -1000000000.0


def nn(a, b):
    return lax.dot_general(a, b, (((1,), (0,)), ((), ())), preferred_element_type=F32)


def nt(a, b):
    return lax.dot_general(a, b, (((1,), (1,)), ((), ())), preferred_element_type=F32)


def tn(a, b):
    return lax.dot_general(a, b, (((0,), (0,)), ((), ())), preferred_element_type=F32)


def ln_stats(x):
    mean = jnp.sum(x, axis=-1, keepdims=True) * (1.0 / x.shape[-1])
    c = x - mean
    var = jnp.sum(c * c, axis=-1, keepdims=True) * (1.0 / x.shape[-1])
    r = lax.rsqrt(var + EPS)
    return c * r, r


def ln_back(dxh, xh, r):
    n = 1.0 / dxh.shape[-1]
    m1 = jnp.sum(dxh, axis=-1, keepdims=True) * n
    m2 = jnp.sum(dxh * xh, axis=-1, keepdims=True) * n
    return r * (dxh - m1 - xh * m2)


def sigmoid(x):
    return 0.5 * jnp.tanh(0.5 * x) + 0.5


def gelu_parts(x):
    c = 0.7978845608028654
    x2 = x * x
    t = jnp.tanh(x * (c + (c * 0.044715) * x2))
    h = 0.5 * x * (1.0 + t)
    d = 0.5 * (1.0 + t) + 0.5 * x * (1.0 - t * t) * (c + (3.0 * c * 0.044715) * x2)
    return h, d


def head_mask(rows, dim=32):
    r = lax.broadcasted_iota(jnp.int32, (rows, PAIR), 0) // (rows // PH)
    l = lax.broadcasted_iota(jnp.int32, (rows, PAIR), 1) // dim
    return r == l


def block_diag(k, mask):
    t = jnp.concatenate([k, k, k, k], axis=0)
    return jnp.where(mask, t, jnp.zeros_like(t))


def seg_max(s, lane_head):
    out = None
    for h in range(PH):
        m = jnp.max(jnp.where(lane_head == h, s, -jnp.inf), axis=-1, keepdims=True)
        out = jnp.broadcast_to(m, s.shape) if out is None else jnp.where(lane_head == h, m, out)
    return out


def fwd_kernel(len_ref, sides_ref, rel_ref, w_op, w_tri, w_to, w_pa, w_po, w_p1, w_p2, w_bb, g_ref,
               bias_ref, p0_ref, p1_ref, p2_ref, p3_ref, tri_ref, gt_ref, pa_ref, hh_ref,
               b_scr, a_scr):
    c = pl.program_id(0)
    length = len_ref[c]
    nchunk = (length + RB - 1) // RB
    g = [g_ref[i:i + 1, :] for i in range(6)]
    jpos = lax.broadcasted_iota(jnp.int32, (RES, PAIR), 0)
    jmask = (jpos < length).astype(F32)
    lane = lax.broadcasted_iota(jnp.int32, (RES, PAIR), 1)
    lane_head = lane // 32
    key_ok = (lane % 32) < length
    hmask = head_mask(PAIR)
    ones_bd = hmask.astype(BF)

    @pl.when(nchunk < RES // RB)
    def _():
        b_scr[...] = jnp.zeros_like(b_scr)
        p0_ref[...] = jnp.zeros_like(p0_ref)
        p1_ref[...] = jnp.zeros_like(p1_ref)
        p2_ref[...] = jnp.zeros_like(p2_ref)
        p3_ref[...] = jnp.zeros_like(p3_ref)
        tri_ref[...] = jnp.zeros_like(tri_ref)
        gt_ref[...] = jnp.zeros_like(gt_ref)
        pa_ref[...] = jnp.zeros_like(pa_ref)
        hh_ref[...] = jnp.zeros_like(hh_ref)
        bias_ref[...] = jnp.zeros_like(bias_ref)

    right = sides_ref[0, :, PAIR:]

    def phase1(ci, _):
        i0 = pl.multiple_of(ci * RB, RB)
        r0 = pl.multiple_of(ci * M, M)
        rows = pl.ds(r0, M)
        left = sides_ref[0, pl.ds(i0, RB), :PAIR]
        outer = (left[:, None, :] * right[None]).reshape(M, PAIR).astype(BF)
        rel = jnp.concatenate([rel_ref[pl.ds(32 - (i0 + k), RES), :] for k in range(RB)], axis=0)
        p0 = nn(outer, w_op[...]) + rel
        p0_ref[0, rows, :] = p0
        xh, _ = ln_stats(p0)
        t = nn((xh * g[0]).astype(BF), w_tri[...])
        ipos = i0 + lax.broadcasted_iota(jnp.int32, (RB, RES, PAIR), 0)
        pm = (jmask[None] * (ipos < length).astype(F32)).reshape(M, PAIR)
        sa = sigmoid(t[:, :PAIR])
        a = (sa * t[:, PAIR:2 * PAIR] * pm).astype(BF)
        sb = sigmoid(t[:, 2 * PAIR:3 * PAIR])
        b = (sb * t[:, 3 * PAIR:4 * PAIR] * pm).astype(BF)
        st = sigmoid(t[:, 4 * PAIR:])
        gt_ref[0, rows, 0:128] = sa.astype(BF)
        gt_ref[0, rows, 128:256] = a
        gt_ref[0, rows, 256:384] = sb.astype(BF)
        gt_ref[0, rows, 384:512] = b
        gt_ref[0, rows, 512:640] = st.astype(BF)
        a_scr[rows, :] = a.astype(F32)
        b_scr[rows, :] = b.astype(F32)
        return 0

    lax.fori_loop(0, nchunk, phase1, 0)

    IB = 4

    def tri_rows(ib, _):
        i0 = ib * IB
        acc = [jnp.zeros((RES, PAIR), F32) for _ in range(IB)]
        for k in range(RES):
            bt = b_scr[pl.ds(k, RES, stride=RES), :]
            for u in range(IB):
                acc[u] = acc[u] + a_scr[pl.ds((i0 + u) * RES + k, 1), :] * bt
        for u in range(IB):
            tri_ref[0, pl.ds(pl.multiple_of((i0 + u) * RES, RES), RES), :] = acc[u]
        return 0

    lax.fori_loop(0, nchunk * (RB // IB), tri_rows, 0)

    def phase2(ci, _):
        r0 = pl.multiple_of(ci * M, M)
        rows = pl.ds(r0, M)
        xt, _ = ln_stats(tri_ref[0, rows, :])
        u = nn((xt * g[1]).astype(BF), w_to[...])
        p1 = p0_ref[0, rows, :] + gt_ref[0, rows, 512:640].astype(F32) * u
        p1_ref[0, rows, :] = p1
        x2, _ = ln_stats(p1)
        pa = nn((x2 * g[2]).astype(BF), w_pa[...])
        qkv = pa[:, :384].astype(BF)
        sg = sigmoid(pa[:, 384:])
        pa_ref[0, rows, 0:384] = qkv
        pa_ref[0, rows, 384:512] = sg.astype(BF)
        outs = []
        for i in range(RB):
            sl = slice(i * RES, (i + 1) * RES)
            kbd = block_diag(qkv[sl, 128:256], hmask)
            s = nt(qkv[sl, :128], kbd) * (32.0 ** -0.5)
            s = jnp.where(key_ok, s, NEG)
            e = jnp.exp(s - seg_max(s, lane_head)).astype(BF)
            rhs = jnp.concatenate([block_diag(qkv[sl, 256:384], hmask), ones_bd], axis=1)
            o2 = nn(e, rhs)
            inv = 1.0 / o2[:, PAIR:]
            o = o2[:, :PAIR] * inv
            outs.append(o)
            pa_ref[0, pl.ds(pl.multiple_of(r0 + i * RES, RES), RES), 512:640] = (e.astype(F32) * inv).astype(BF)
        o = jnp.concatenate(outs, axis=0)
        pa_ref[0, rows, 640:768] = o.astype(BF)
        p2 = p1 + nn((sg * o).astype(BF), w_po[...])
        p2_ref[0, rows, :] = p2
        x3, _ = ln_stats(p2)
        hpre = nn((x3 * g[3]).astype(BF), w_p1[...])
        h, hd = gelu_parts(hpre)
        hb = h.astype(BF)
        hh_ref[0, rows, 0:512] = hb
        hh_ref[0, rows, 512:1024] = hd.astype(BF)
        p3 = p2 + nn(hb, w_p2[...])
        p3_ref[0, rows, :] = p3
        x4, _ = ln_stats(p3)
        xx = jnp.concatenate([(x4 * g[4]).astype(BF), (x4 * g[5]).astype(BF)], axis=1)
        bias_ref[0, :, rows] = nt(w_bb[...], xx)
        return 0

    lax.fori_loop(0, nchunk, phase2, 0)


def full(shape):
    n = len(shape)
    return pl.BlockSpec(shape, lambda c, *_: (0,) * n)


def per_crop(shape):
    n = len(shape)
    return pl.BlockSpec((1,) + shape, lambda c, *_: (c,) + (0,) * n)


def pair_forward(lengths, sides, rel, w_op, w_tri, w_to, w_pa, w_po, w_p1, w_p2, w_bb, gains):
    crops = sides.shape[0]
    n = RES * RES
    outs = [((16, n), F32), ((n, 128), F32), ((n, 128), F32), ((n, 128), F32), ((n, 128), F32), ((n, 128), F32),
            ((n, 640), BF), ((n, 768), BF), ((n, 1024), BF)]
    ws = [rel, w_op, w_tri, w_to, w_pa, w_po, w_p1, w_p2, w_bb, gains]
    return pl.pallas_call(
        fwd_kernel,
        grid_spec=pltpu.PrefetchScalarGridSpec(
            num_scalar_prefetch=1,
            grid=(crops,),
            in_specs=[per_crop((RES, 256))] + [full(w.shape) for w in ws],
            out_specs=[per_crop(s) for s, _ in outs],
            scratch_shapes=[pltpu.VMEM((n, 128), F32), pltpu.VMEM((n, 128), F32)],
        ),
        out_shape=[jax.ShapeDtypeStruct((crops,) + s, d) for s, d in outs],
        compiler_params=pltpu.CompilerParams(vmem_limit_bytes=58 << 20),
        name="pair_fwd",
    )(lengths, sides, *ws)


def bwd_kernel(len_ref, dbt_ref, db_ref, sides_ref, p0_ref, p1_ref, p2_ref, p3_ref, tri_ref, gt_ref, pa_ref, hh_ref,
               w_op, w_tri, w_to, w_pa, w_po, w_p1, w_p2, w_bb, g_ref,
               dsides_ref, d_op, d_tri, d_to, d_pa, d_po, d_p1, d_p2t, d_bb, d_g, d_rel,
               a_scr, b_scr, dt_scr, dp_scr, dtg_scr):
    c = pl.program_id(0)
    length = len_ref[c]
    nchunk = (length + RB - 1) // RB
    g = [g_ref[i:i + 1, :] for i in range(6)]
    lane = lax.broadcasted_iota(jnp.int32, (RES, PAIR), 1)
    hmask = head_mask(PAIR)
    ones_bd = hmask.astype(BF)

    @pl.when(c == 0)
    def _():
        for ref in (d_op, d_tri, d_to, d_pa, d_po, d_p1, d_p2t, d_bb, d_g, d_rel):
            ref[...] = jnp.zeros_like(ref)

    dsides_ref[...] = jnp.zeros_like(dsides_ref)

    @pl.when(nchunk < RES // RB)
    def _():
        dt_scr[...] = jnp.zeros_like(dt_scr)
        a_scr[...] = jnp.zeros_like(a_scr)
        b_scr[...] = jnp.zeros_like(b_scr)

    def gain_add(i, v):
        d_g[i * 8:(i + 1) * 8, :] += jnp.sum(v.reshape(M // 8, 8, PAIR), axis=0)

    def phase_a(ci, _):
        r0 = pl.multiple_of(ci * M, M)
        rows = pl.ds(r0, M)
        x4, r4 = ln_stats(p3_ref[0, rows, :])
        xx = jnp.concatenate([(x4 * g[4]).astype(BF), (x4 * g[5]).astype(BF)], axis=1)
        d_bb[...] += nn(dbt_ref[0, :, rows], xx)
        dxx = nn(db_ref[0, rows, :], w_bb[...])
        da, di = dxx[:, :PAIR], dxx[:, PAIR:]
        gain_add(4, da * x4)
        gain_add(5, di * x4)
        dp = ln_back(da * g[4] + di * g[5], x4, r4)
        dpb = dp.astype(BF)
        d_p2t[...] += tn(dpb, hh_ref[0, rows, 0:512])
        dh = nt(dpb, w_p2[...])
        dhb = (dh * hh_ref[0, rows, 512:1024].astype(F32)).astype(BF)
        x3, r3 = ln_stats(p2_ref[0, rows, :])
        d_p1[...] += tn((x3 * g[3]).astype(BF), dhb)
        dx = nt(dhb, w_p1[...])
        gain_add(3, dx * x3)
        dp = dp + ln_back(dx * g[3], x3, r3)
        dpb = dp.astype(BF)
        sg = pa_ref[0, rows, 384:512].astype(F32)
        o = pa_ref[0, rows, 640:768].astype(F32)
        so = sg * o
        d_po[...] += tn(so.astype(BF), dpb)
        dy = nt(dpb, w_po[...])
        do = dy * sg
        dsg = dy * so * (1.0 - sg)
        dob = do.astype(BF)
        delta = nn((do * o).astype(BF), ones_bd)
        dqkv = []
        for i in range(RB):
            sl = slice(i * RES, (i + 1) * RES)
            ri = pl.ds(pl.multiple_of(r0 + i * RES, RES), RES)
            q = pa_ref[0, ri, 0:128]
            kbd = block_diag(pa_ref[0, ri, 128:256], hmask)
            vbd = block_diag(pa_ref[0, ri, 256:384], hmask)
            p = pa_ref[0, ri, 512:640]
            dpr = nt(dob[sl], vbd)
            ds = (p.astype(F32) * (dpr - delta[sl]) * (32.0 ** -0.5)).astype(BF)
            dq = nn(ds, kbd)
            both = jnp.concatenate([ds, p], axis=1)
            t = tn(both, jnp.concatenate([q, dob[sl]], axis=1))
            dkb = jnp.where(hmask, t[:PAIR, :PAIR], 0.0)
            dvb = jnp.where(hmask, t[PAIR:, PAIR:], 0.0)
            dk = dkb[0:32] + dkb[32:64] + dkb[64:96] + dkb[96:128]
            dv = dvb[0:32] + dvb[32:64] + dvb[64:96] + dvb[96:128]
            dqkv.append(jnp.concatenate([dq.astype(BF), dk.astype(BF), dv.astype(BF)], axis=1))
        dpa = jnp.concatenate([jnp.concatenate(dqkv, axis=0), dsg.astype(BF)], axis=1)
        x2, r2 = ln_stats(p1_ref[0, rows, :])
        d_pa[...] += tn((x2 * g[2]).astype(BF), dpa)
        dx = nt(dpa, w_pa[...])
        gain_add(2, dx * x2)
        dp = dp + ln_back(dx * g[2], x2, r2)
        dp_scr[rows, :] = dp
        xt, rt = ln_stats(tri_ref[0, rows, :])
        xtb = (xt * g[1]).astype(BF)
        u = nn(xtb, w_to[...])
        st = gt_ref[0, rows, 512:640].astype(F32)
        du = dp * st
        dtg_scr[rows, :] = (du * u * (1.0 - st)).astype(BF)
        dub = du.astype(BF)
        d_to[...] += tn(xtb, dub)
        dx = nt(dub, w_to[...])
        gain_add(1, dx * xt)
        dt_scr[rows, :] = ln_back(dx * g[1], xt, rt)
        a_scr[rows, :] = gt_ref[0, rows, 128:256].astype(F32)
        b_scr[rows, :] = gt_ref[0, rows, 384:512].astype(F32)
        return 0

    lax.fori_loop(0, nchunk, phase_a, 0)

    right = sides_ref[0, :, PAIR:]
    IB = 4

    def phase_c(ci, _):
        i0 = pl.multiple_of(ci * RB, RB)
        r0 = pl.multiple_of(ci * M, M)
        rows = pl.ds(r0, M)
        das, dbs = [], []
        for blk in range(RB // IB):
            acc = [jnp.zeros((RES, PAIR), F32) for _ in range(IB)]
            for j in range(RES):
                bj = b_scr[j * RES:(j + 1) * RES, :]
                for u in range(IB):
                    acc[u] = acc[u] + dt_scr[pl.ds((i0 + blk * IB + u) * RES + j, 1), :] * bj
            das += acc
            acc = [jnp.zeros((RES, PAIR), F32) for _ in range(IB)]
            for i in range(RES):
                ai = a_scr[i * RES:(i + 1) * RES, :]
                for u in range(IB):
                    acc[u] = acc[u] + dt_scr[pl.ds(i * RES + i0 + blk * IB + u, 1), :] * ai
            dbs += acc
        da = jnp.concatenate(das, axis=0)
        db = jnp.concatenate(dbs, axis=0)
        jpos = lax.broadcasted_iota(jnp.int32, (RB, RES, PAIR), 1)
        ipos = i0 + lax.broadcasted_iota(jnp.int32, (RB, RES, PAIR), 0)
        pm = ((jpos < length) & (ipos < length)).astype(F32).reshape(M, PAIR)
        sa = gt_ref[0, rows, 0:128].astype(F32)
        sb = gt_ref[0, rows, 256:384].astype(F32)
        a = a_scr[rows, :]
        b = b_scr[rows, :]
        dt = jnp.concatenate([
            (da * a * (1.0 - sa)).astype(BF), (da * sa * pm).astype(BF),
            (db * b * (1.0 - sb)).astype(BF), (db * sb * pm).astype(BF), dtg_scr[rows, :]], axis=1)
        x0, rr = ln_stats(p0_ref[0, rows, :])
        d_tri[...] += tn((x0 * g[0]).astype(BF), dt)
        dx = nt(dt, w_tri[...])
        gain_add(0, dx * x0)
        dp = dp_scr[rows, :] + ln_back(dx * g[0], x0, rr)
        for k in range(RB):
            sl = pl.ds(32 - (i0 + k), RES)
            d_rel[sl, :] += dp[k * RES:(k + 1) * RES]
        dpb = dp.astype(BF)
        left = sides_ref[0, pl.ds(i0, RB), :PAIR]
        outer = (left[:, None, :] * right[None]).reshape(M, PAIR).astype(BF)
        d_op[...] += tn(outer, dpb)
        do = nt(dpb, w_op[...]).reshape(RB, RES, PAIR)
        dsides_ref[0, pl.ds(i0, RB), :PAIR] = jnp.sum(do * right[None], axis=1)
        dsides_ref[0, :, PAIR:] += jnp.sum(do * left[:, None, :], axis=0)
        return 0

    lax.fori_loop(0, nchunk, phase_c, 0)


def pair_backward(lengths, dbt, db, sides, res, w_op, w_tri, w_to, w_pa, w_po, w_p1, w_p2, w_bb, gains):
    crops = sides.shape[0]
    n = RES * RES
    ws = [w_op, w_tri, w_to, w_pa, w_po, w_p1, w_p2, w_bb, gains]
    outs = [(128, 128), (128, 640), (128, 128), (128, 512), (128, 128), (128, 512), (128, 512), (16, 256), (48, 128), (72, 128)]
    ins = [dbt, db, sides, *res]
    return pl.pallas_call(
        bwd_kernel,
        grid_spec=pltpu.PrefetchScalarGridSpec(
            num_scalar_prefetch=1,
            grid=(crops,),
            in_specs=[per_crop(x.shape[1:]) for x in ins] + [full(w.shape) for w in ws],
            out_specs=[per_crop((RES, 256))] + [full(s) for s in outs],
            scratch_shapes=[pltpu.VMEM((n, 128), F32)] * 4 + [pltpu.VMEM((n, 128), BF)],
        ),
        out_shape=[jax.ShapeDtypeStruct((crops, RES, 256), F32)] + [jax.ShapeDtypeStruct(s, F32) for s in outs],
        compiler_params=pltpu.CompilerParams(vmem_limit_bytes=58 << 20),
        name="pair_bwd",
    )(lengths, *ins, *ws)

@jax.custom_vjp
def pair_stack(lengths, sides, pp):
    return pair_run(lengths, sides, pp)[0]


def pair_operands(pp):
    low = {k: v.astype(BF) for k, v in pp.items()}
    zero = jnp.zeros((HEADS, PAIR), BF)
    w_bb = jnp.concatenate(
        [
            jnp.concatenate([low["w_bias"].T, zero], axis=1),
            jnp.concatenate([zero, low["w_ipa_bias"].T], axis=1),
        ],
        axis=0,
    )
    names = ("w_op", "w_tri", "w_tri_out", "w_pa", "w_pa_out", "w_p1", "w_p2")
    return [low[k] for k in names] + [w_bb, pp["g_pair"]]


def pair_run(lengths, sides, pp):
    rel = jnp.pad(pp["w_rel"], ((0, 7), (0, 0)))
    ops = pair_operands(pp)
    both, *res = pair_forward(lengths, sides, rel, *ops)
    return both, (lengths, sides, res, ops)


def pair_back(saved, d_both):
    lengths, sides, res, ops = saved
    d = d_both.astype(BF)
    ds, d_op, d_tri, d_to, d_pa, d_po, d_p1, d_p2t, d_bb, d_g, d_rel = pair_backward(
        lengths, d, jnp.swapaxes(d, 1, 2), sides, res, *ops
    )
    grads = {
        "w_op": d_op,
        "w_tri": d_tri,
        "w_tri_out": d_to,
        "w_pa": d_pa,
        "w_pa_out": d_po,
        "w_p1": d_p1,
        "w_p2": d_p2t.T,
        "w_rel": d_rel[:BINS],
        "w_bias": d_bb[:HEADS, :PAIR].T,
        "w_ipa_bias": d_bb[HEADS:, PAIR:].T,
        "g_pair": d_g.reshape(6, 8, PAIR).sum(1),
    }
    return None, ds, grads


pair_stack.defvjp(pair_run, pair_back)

PAIR_NAMES = ("w_op", "w_tri", "w_tri_out", "w_pa", "w_pa_out", "w_p1", "w_p2", "w_rel", "w_bias", "w_ipa_bias", "g_pair")


def frozen_plm(table, uvz_table, plm_second, tokens, lengths):
    crops, residues = tokens.shape
    one_hot = (tokens[:, :, None] == jnp.arange(VOCAB)[None, None, :]).astype(BF)
    key_mask = (jnp.arange(residues)[None, :] < lengths[:, None])[:, None, :]
    features = product("crv,vp->crp", one_hot, table)
    base = jnp.einsum("crv,vz->crz", one_hot, uvz_table[:, 2 * PLM_FF :].astype(BF))
    gate = jnp.einsum("crv,vz->crz", one_hot.astype(F32), uvz_table[:, :PLM_FF], precision=lax.Precision.HIGHEST)
    value = jnp.einsum("crv,vz->crz", one_hot, uvz_table[:, PLM_FF : 2 * PLM_FF].astype(BF))
    scores = jnp.where(key_mask, product("ciz,cjz->cij", base, base) * PLM_Z ** (-0.5), NEG)
    mixed = product("cij,cje->cie", softmax_last(scores), value)
    plm_out = features + product("cie,ep->cip", gate * mixed, plm_second)
    return layer_norm(plm_out, 1.0).astype(BF)


def crop_loss(params, plm_low, lengths, weight_res, valid, coords):
    multiply = product
    crops, residues = weight_res.shape
    node = multiply("crp,pn->crn", plm_low, params["w_in"])
    gain_node = params["g_node"]
    sides = multiply("crn,nq->crq", layer_norm(node, gain_node[0]), params["w_lr"])
    both = pair_stack(lengths, sides, {k: params[k] for k in PAIR_NAMES})
    both = both.reshape(crops, 2, HEADS, residues, residues)
    bias, ipa_bias = both[:, 0], both[:, 1]
    head_dim = NODE // HEADS
    qkv = (
        multiply("crn,nq->crq", (layer_norm(node, gain_node[1])), params["w_qkv"])
    )
    query = qkv[..., :NODE].reshape(crops, residues, HEADS, head_dim)
    keys = qkv[..., NODE : 2 * NODE].reshape(crops, residues, HEADS, head_dim)
    values = qkv[..., 2 * NODE :].reshape(crops, residues, HEADS, head_dim)
    scores = multiply("cihd,cjhd->chij", query, keys) * head_dim ** (-0.5) + bias
    scores = jnp.where(valid[:, None, None, :] > 0, scores, -1000000000.0)
    attended = multiply("chij,cjhd->cihd", (softmax_last(scores)), values).reshape(
        crops, residues, NODE
    )
    node = node + multiply("crn,nm->crm", (attended), params["w_out"])
    hidden_node = jax.nn.gelu(
        multiply("crn,nf->crf", (layer_norm(node, gain_node[2])), params["w_n1"]),
        approximate=True,
    )
    node = node + multiply("crf,fn->crn", (hidden_node), params["w_n2"])
    start_pos = multiply("crn,nk->crk", (layer_norm(node, gain_node[3])), params["w_s"])
    single = (layer_norm(node, gain_node[4]))
    sqkv = (multiply("crn,nq->crq", single, params["w_ipa"]))
    s_query = sqkv[..., :NODE].reshape(crops, residues, HEADS, head_dim)
    s_keys = sqkv[..., NODE : 2 * NODE].reshape(crops, residues, HEADS, head_dim)
    s_values = sqkv[..., 2 * NODE :].reshape(crops, residues, HEADS, head_dim)
    points = (multiply("crn,nq->crq", single, params["w_pts"])).reshape(
        crops, residues, 2, HEADS, IPA_PTS, 3
    )
    points = points + start_pos[:, :, None, None, None, :]
    point_diff = points[:, :, None, 0] - points[:, None, :, 1]
    dist = jnp.transpose(jnp.sum(point_diff * point_diff, axis=(-1, -2)), (0, 3, 1, 2))
    ipa_scores = (
        multiply("cihd,cjhd->chij", s_query, s_keys) * head_dim ** (-0.5)
        + ipa_bias
        - point_weight * dist
    )
    ipa_scores = jnp.where(valid[:, None, None, :] > 0, ipa_scores, -1000000000.0)
    ipa_att = multiply("chij,cjhd->cihd", (softmax_last(ipa_scores)), s_values).reshape(
        crops, residues, NODE
    )
    node = node + multiply("crn,nm->crm", (ipa_att), params["w_ipa_out"])
    predicted = start_pos + multiply(
        "crn,nk->crk", (layer_norm(node, gain_node[5])), params["w_bb"]
    )
    truth = jnp.transpose(coords, (0, 2, 1))
    pred_diff = predicted[:, :, None, :] - predicted[:, None, :, :]
    true_diff = truth[:, :, None, :] - truth[:, None, :, :]
    dist_pred = jnp.sqrt(jnp.sum(pred_diff * pred_diff, axis=-1) + 1.0)
    dist_true = jnp.sqrt(jnp.sum(true_diff * true_diff, axis=-1) + 1.0)
    error = jnp.sqrt((dist_pred - dist_true) ** 2 + 1.0) - 1.0
    pair_weight = weight_res[:, :, None] * weight_res[:, None, :]
    return jnp.sum(pair_weight * error)


def adam_update(master, first_moment, second_moment, step, grad, norm):
    clipped = grad * jnp.minimum(1.0, clip_norm / norm)
    first = beta_one * first_moment + (1.0 - beta_one) * clipped
    second = beta_two * second_moment + (1.0 - beta_two) * clipped * clipped
    step_count = step[0].astype(jnp.float32)
    first_hat = first / (1.0 - beta_one**step_count)
    second_hat = second / (1.0 - beta_two**step_count)
    updated = master - learn_rate * (
        first_hat / (jnp.sqrt(second_hat) + adam_eps) + decay_rate * master
    )
    return (updated, first, second, updated.astype(jnp.bfloat16))


def local(
    master,
    first_moment,
    second_moment,
    step,
    plm_table,
    plm_first,
    plm_second,
    tokens,
    lengths,
    resolved,
    coords,
):
    table_low = layer_norm(plm_table.astype(F32), 1.0).astype(BF)
    depth = plm_first.shape[0]
    own_table = lax.dynamic_slice_in_dim(table_low, lax.axis_index("shard") * depth, depth, 1)
    uvz_table = jax.nn.silu(lax.psum(product("vp,pe->ve", own_table, plm_first), "shard"))
    frozen_second = lax.all_gather(plm_second, "shard", axis=0, tiled=True)
    gathered = lax.all_gather(master.astype(BF), "shard", axis=0, tiled=True)
    params = unpack(gathered.astype(F32).reshape(-1))
    weight_res, valid = residue_weight(lengths, resolved)
    local_pairs = jnp.sum(jnp.sum(weight_res, axis=1) ** 2)
    plm_low = frozen_plm(plm_table, uvz_table, frozen_second, tokens, lengths)

    def loss_of(weights):
        return crop_loss(weights, plm_low, lengths, weight_res, valid, coords)

    loss_part, pullback = jax.vjp(loss_of, params)
    (grads,) = pullback(jnp.float32(1.0))
    flat = jnp.concatenate([grads[name].reshape(-1) for name, extent in layout()])
    spare = gathered.size - flat.shape[0]
    scalars = jnp.pad(jnp.stack([loss_part, local_pairs]), (0, spare - 2))
    summed = lax.psum(jnp.concatenate([flat, scalars]).reshape(-1, 128), ("crop", "shard"))
    inv_count = 1.0 / summed[-1, 1]
    loss = summed[-1, 0] * inv_count
    live = (jnp.arange(summed.shape[0]) < summed.shape[0] - spare // 128)[:, None]
    summed = jnp.where(live, summed * inv_count, 0.0)
    own_rows = master.shape[0]
    own_grad = lax.dynamic_slice_in_dim(summed, lax.axis_index("shard") * own_rows, own_rows, 0)
    norm = jnp.sqrt(jnp.sum(summed * summed))
    updated, first, second, copy_low = adam_update(
        master, first_moment, second_moment, step, own_grad, norm
    )
    return (updated, first, second, copy_low, loss, norm)


def solution(mesh):
    placed = (
        P("shard", None),
        P("shard", None),
        P("shard", None),
        P(),
        P(),
        P("shard", None),
        P("shard", None),
        P(("crop", "shard"), None),
        P(("crop", "shard")),
        P(("crop", "shard"), None),
        P(("crop", "shard"), None, None),
    )
    return jax.shard_map(
        local,
        mesh=mesh,
        in_specs=placed,
        out_specs=(
            P("shard", None),
            P("shard", None),
            P("shard", None),
            P("shard", None),
            P(),
            P(),
        ),
        check_vma=False,
    )
```
